128 devices in a mesh: wide: 16 (over x, y), narrow: 8 (over z, core).
Axes of the slice: x: 4, y: 4, z: 4, core: 2. Of those that a mesh axis runs over, the one named last changes fastest.
Arguments:
- loads: bfloat16 [256, 524288], P('narrow', 'wide'), may hold values from -6 to 6
- state: bfloat16 [256, 524288], P('narrow', 'wide'), may hold values from -6 to 6
- modal_diag: float32 [524288], P('wide'), may hold values from 0.5 to 2
- phi: bfloat16 [4096, 128, 128], P('wide'), may hold values from -0.25 to 0.25
- incidence: int32 [4096], P('wide'), may hold values from 0 to 127
- sizes: int32 [2048], P('wide'), may hold values from 1 to 129, as said below
- factor: float32 [16384, 16384], P('wide', 'narrow'), may hold values from -0.046875 to 0.046875
Outputs:
- adjoint: bfloat16 [256, 524288], P('narrow', 'wide')
- sensitivity: float32 [256, 2048], P('narrow', 'wide')
The draws below stay inside these ranges and needn't reach their ends.
Inputs may be any that keep to these rules, and one draw needn't show every extreme that they name: `sizes`: the 128 substructures of each group hold at most 256 tiles together, and in every draw some group holds exactly 256.
All inputs are finite; a program needn't handle non-finite values.
Results may differ from the reference program's by a relative error of at most 0.015.
Values may be sent and summed in bfloat16 or wider, within the bound.
No kernel may reach another device: no remote copies, remote signals or barrier semaphores. Data moves between devices by JAX's collectives and lax.ppermute only.
A program may use at most 128 MiB of HBM per device.

```python
import math
import jax
import jax.numpy as jnp
from jax import lax

MODES = 16384
BLOCK = 128
LOADS = 256
SUBS_DEV = 128
TILES_DEV = 256
SUBS = 2048
TILES = 4096
ROWS = 524288
MBLOCKS = 128


def draw_sizes(key, part):
    groups = SUBS // SUBS_DEV
    spare = TILES_DEV - SUBS_DEV
    first_key, second_key, third_key, fourth_key = jax.random.split(jax.random.fold_in(key, 7), 4)
    extra = jax.random.randint(first_key, (groups,), 0, spare + 1)
    fullest = jax.random.randint(second_key, (), 0, groups)
    heaviest = jax.random.randint(fourth_key, (), 0, SUBS_DEV)
    is_full = jnp.arange(groups) == fullest
    extra = jnp.where(is_full, spare, extra)
    targets = jax.random.randint(third_key, (groups, spare), 0, SUBS_DEV)
    targets = jnp.where(is_full[:, None], heaviest, targets)
    used = jnp.arange(spare)[None, :] < extra[:, None]
    hits = (targets[:, :, None] == jnp.arange(SUBS_DEV)[None, None, :]) & used[:, :, None]
    counts = jnp.sum(hits.astype(jnp.int32), axis=1)
    return (1 + counts).reshape(groups * SUBS_DEV).astype(jnp.int32)


def with_ends(result, own_key, low, top_value):
    longest = result.shape.index(max(result.shape))
    spots = []
    for shift in (0, 1):
        where = [jax.random.randint(jax.random.fold_in(own_key, axis), (), 0, length) for axis, length in enumerate(result.shape)]
        where[longest] = (where[longest] + shift) % result.shape[longest]
        spots.append(tuple(where))
    return result.at[spots[0]].set(low).at[spots[1]].set(top_value)


def steps_of(key, dims, shards, smallest, top_value):
    level = 1.0
    for position, shards_of in shards:
        steps = jax.random.uniform(jax.random.fold_in(jax.random.fold_in(key, 6), position), (shards_of,), jnp.float32, smallest / len(shards), top_value / len(shards))
        level = level * jnp.repeat(jnp.exp(steps), dims[position] // shards_of).reshape((-1,) + (1,) * (len(dims) - 1 - position))
    return level


def bell_draw(own_key, extent, spread, most, pieces=(), kind=jnp.bfloat16):
    factor_of = steps_of(own_key, extent, pieces, -0.22, 0.18) if pieces else 1.0
    drawn = jax.random.normal(own_key, extent, jnp.float32) * spread * factor_of
    return jnp.minimum(jnp.maximum(drawn, -most), most).astype(kind)


def setup_inputs(seed: int = 0) -> dict:
    keys = jax.random.split(jax.random.key(seed), 8)
    return {
        "loads": bell_draw(keys[0], (LOADS, ROWS), 1.0, 6.0, ((0, 8), (1, 16))),
        "state": bell_draw(keys[1], (LOADS, ROWS), 1.0, 6.0, ((0, 8), (1, 16))),
        "modal_diag": jnp.clip(jnp.exp(math.log(2.0) - 1.3862944 * jax.random.uniform(keys[2], (ROWS,), jnp.float32) ** steps_of(keys[2], (ROWS,), ((0, 16),), -0.2, 0.2)), 0.5, 2.0),
        "phi": bell_draw(keys[3], (TILES, BLOCK, BLOCK), (4 * BLOCK) ** -0.5, 0.25, ((0, 16),)),
        "incidence": with_ends(jax.random.randint(keys[4], (TILES,), 0, MBLOCKS), jax.random.fold_in(keys[4], 1), 0, MBLOCKS - 1).astype(jnp.int32),
        "sizes": draw_sizes(jax.random.fold_in(keys[7], 71), 0),
        "factor": bell_draw(keys[6], (MODES, MODES), MODES ** -0.5, 0.046875, ((0, 16), (1, 8)), jnp.float32),
    }


sens_scale = 0.0625


def reference(loads, state, modal_diag, phi, incidence, sizes, factor):
    groups = SUBS // SUBS_DEV
    block_count = MODES // BLOCK
    load_tiles = loads.reshape(LOADS, groups, TILES_DEV, BLOCK).transpose(1, 0, 2, 3)
    state_tiles = state.reshape(LOADS, groups, TILES_DEV, BLOCK).transpose(1, 0, 2, 3)
    diag_tiles = modal_diag.reshape(groups, TILES_DEV, BLOCK)
    phi_tiles = phi.reshape(groups, TILES_DEV, BLOCK, BLOCK)
    block_ids = incidence.reshape(groups, TILES_DEV)
    group_sizes = sizes.reshape(groups, SUBS_DEV)
    slot_index = jnp.arange(TILES_DEV, dtype=jnp.int32)

    def layout(group_size):
        running = jnp.cumsum(group_size)
        owner_sub = jnp.sum((running[None, :] <= slot_index[:, None]).astype(jnp.int32), axis=1)
        live_slot = slot_index < running[-1]
        return owner_sub, live_slot

    def condense(carry, item):
        load_part, phi_part, id_part, size_part = item
        owner_sub, live_slot = layout(size_part)
        tile_terms = jnp.einsum("lti,tim->tlm", load_part.astype(jnp.float32), phi_part.astype(jnp.float32))
        tile_terms = jnp.where(live_slot[:, None, None], tile_terms, jnp.zeros_like(tile_terms))
        summed = jax.ops.segment_sum(tile_terms, id_part, num_segments=block_count)
        return carry + summed, None

    start_sum = jnp.zeros((block_count, LOADS, BLOCK), jnp.float32)
    blocks_sum, _ = lax.scan(condense, start_sum, (load_tiles, phi_tiles, block_ids, group_sizes))
    condensed = blocks_sum.transpose(1, 0, 2).reshape(LOADS, MODES)
    image = jnp.dot(condensed, factor, precision=lax.Precision.HIGHEST)
    amplitude = jnp.dot(image, factor.T, precision=lax.Precision.HIGHEST)
    amp_round = amplitude.astype(jnp.bfloat16).reshape(LOADS, block_count, BLOCK)

    def recover(item):
        load_part, state_part, diag_part, phi_part, id_part, size_part = item
        owner_sub, live_slot = layout(size_part)
        picked = jnp.take(amp_round, id_part, axis=1).astype(jnp.float32)
        coupling = jnp.einsum("ltm,tim->lti", picked, phi_part.astype(jnp.float32))
        response = diag_part[None, :, :] * load_part.astype(jnp.float32) + coupling
        response = jnp.where(live_slot[None, :, None], response, jnp.zeros_like(response))
        row_totals = jnp.sum(response * state_part.astype(jnp.float32), axis=2) * sens_scale
        member = (owner_sub[:, None] == jnp.arange(SUBS_DEV, dtype=jnp.int32)[None, :]) & live_slot[:, None]
        sensitivity = jnp.dot(row_totals, member.astype(jnp.float32), precision=lax.Precision.HIGHEST)
        return response.astype(jnp.bfloat16), sensitivity

    adjoint_parts, sens_parts = lax.map(recover, (load_tiles, state_tiles, diag_tiles, phi_tiles, block_ids, group_sizes))
    adjoint = adjoint_parts.transpose(1, 0, 2, 3).reshape(LOADS, ROWS)
    sensitivity = sens_parts.transpose(1, 0, 2).reshape(LOADS, SUBS)
    return (adjoint, sensitivity)
```

```python
import jax
import jax.numpy as jnp
from jax import lax
from jax.experimental import pallas as pl
from jax.experimental.pallas import tpu as pltpu
from jax.sharding import Mesh, PartitionSpec as P

sens_scale = 0.0625
BLOCK = 128
WIDE = ("x", "y")
F32, BF16 = jnp.float32, jnp.bfloat16


def condense(inc, sizes, loads, phi, factor, peers, steps):
    load_cols = loads.shape[0]
    tiles = phi.shape[0]
    subs = sizes.shape[0]
    frows, fcols = factor.shape
    blocks = peers * frows // BLOCK
    per_step = tiles // steps

    def kernel(inc_ref, sizes_ref, loads_ref, phi_ref, f_ref, out_ref, fb_ref, acc_ref, live_ref):
        step = pl.program_id(0)

        @pl.when(step == 0)
        def _():
            acc_ref[...] = jnp.zeros_like(acc_ref)
            live_ref[0] = lax.fori_loop(0, subs, lambda s, n: n + sizes_ref[s], jnp.int32(0))

        live = live_ref[0]
        for j in range(per_step):
            tile = step * per_step + j
            term = jnp.dot(loads_ref[:, j * BLOCK : (j + 1) * BLOCK], phi_ref[j], preferred_element_type=F32)
            term = jnp.where(tile < live, term, jnp.zeros_like(term))
            acc_ref[inc_ref[tile]] += term
        fb_ref[...] = f_ref[...].astype(BF16)

        @pl.when(step == steps - 1)
        def _():
            per = blocks // peers
            for b in range(blocks):
                out_ref[b // per, :, (b % per) * BLOCK : (b % per + 1) * BLOCK] = acc_ref[b].astype(BF16)

    return pl.pallas_call(
        kernel,
        out_shape=(
            jax.ShapeDtypeStruct((peers, load_cols, frows), BF16),
            jax.ShapeDtypeStruct((frows, fcols), BF16),
        ),
        grid_spec=pltpu.PrefetchScalarGridSpec(
            num_scalar_prefetch=2,
            grid=(steps,),
            in_specs=[
                pl.BlockSpec((load_cols, per_step * BLOCK), lambda i, *_: (0, i)),
                pl.BlockSpec((per_step, BLOCK, BLOCK), lambda i, *_: (i, 0, 0)),
                pl.BlockSpec((frows // steps, fcols), lambda i, *_: (i, 0)),
            ],
            out_specs=(
                pl.BlockSpec((peers, load_cols, frows), lambda i, *_: (0, 0, 0)),
                pl.BlockSpec((frows // steps, fcols), lambda i, *_: (i, 0)),
            ),
            scratch_shapes=[
                pltpu.VMEM((blocks, load_cols, BLOCK), F32),
                pltpu.SMEM((1,), jnp.int32),
            ],
        ),
        compiler_params=pltpu.CompilerParams(vmem_limit_bytes=40 << 20),
        name="condense",
    )(inc, sizes, loads, phi, factor)


def times_factor(left, own, other, steps):
    rows, depth = left.shape
    cols = own.shape[1]
    width = cols // steps

    def kernel(left_ref, own_ref, other_ref, out_ref):
        step = pl.program_id(0)

        @pl.when(step < steps)
        def _():
            out_ref[...] = jnp.dot(left_ref[...], own_ref[...], preferred_element_type=F32).astype(BF16)

        @pl.when(step >= steps)
        def _():
            out_ref[...] = jnp.dot(left_ref[...], other_ref[...], preferred_element_type=F32).astype(BF16)

    return pl.pallas_call(
        kernel,
        out_shape=jax.ShapeDtypeStruct((rows, 2 * cols), BF16),
        grid=(2 * steps,),
        in_specs=[
            pl.BlockSpec((rows, depth), lambda i: (0, 0)),
            pl.BlockSpec((depth, width), lambda i: (0, jnp.minimum(i, steps - 1))),
            pl.BlockSpec((depth, width), lambda i: (0, jnp.maximum(i - steps, 0))),
        ],
        out_specs=pl.BlockSpec((rows, width), lambda i: (0, i)),
        compiler_params=pltpu.CompilerParams(vmem_limit_bytes=40 << 20),
        name="times_factor",
    )(left, own, other)


def times_transpose(image, own, other, steps):
    rows = image.shape[0]
    frows, cols = own.shape
    height = frows // steps
    contract = (((1,), (1,)), ((), ()))

    def kernel(image_ref, own_ref, other_ref, out_ref):
        total = lax.dot_general(image_ref[:, :cols], own_ref[...], contract, preferred_element_type=F32)
        total += lax.dot_general(image_ref[:, cols:], other_ref[...], contract, preferred_element_type=F32)
        out_ref[...] = total.astype(BF16)

    return pl.pallas_call(
        kernel,
        out_shape=jax.ShapeDtypeStruct((rows, frows), BF16),
        grid=(steps,),
        in_specs=[
            pl.BlockSpec((rows, 2 * cols), lambda i: (0, 0)),
            pl.BlockSpec((height, cols), lambda i: (i, 0)),
            pl.BlockSpec((height, cols), lambda i: (i, 0)),
        ],
        out_specs=pl.BlockSpec((rows, height), lambda i: (0, i)),
        compiler_params=pltpu.CompilerParams(vmem_limit_bytes=40 << 20),
        name="times_transpose",
    )(image, own, other)


def recover(inc, sizes, amp, loads, state, diag, phi, steps):
    load_cols = loads.shape[0]
    tiles = phi.shape[0]
    subs = sizes.shape[0]
    peers, _, frows = amp.shape
    per = frows // BLOCK
    blocks = peers * per
    per_step = tiles // steps
    contract = (((1,), (1,)), ((), ()))

    def kernel(inc_ref, sizes_ref, amp_ref, loads_ref, state_ref, diag_ref, phi_ref, adj_ref, sens_ref, blk_ref, at_ref):
        step = pl.program_id(0)

        @pl.when(step == 0)
        def _():
            for b in range(blocks):
                blk_ref[b] = amp_ref[b // per, :, (b % per) * BLOCK : (b % per + 1) * BLOCK]
            sens_ref[...] = jnp.zeros_like(sens_ref)
            at_ref[0] = 0
            at_ref[1] = sizes_ref[0]

        lane = lax.broadcasted_iota(jnp.int32, (load_cols, subs), 1)
        owner = at_ref[0]
        end = at_ref[1]
        sens = sens_ref[...]
        for j in range(per_step):
            tile = step * per_step + j
            past = (tile >= end) & (owner < subs)
            owner = jnp.where(past, owner + 1, owner)
            end = jnp.where(past & (owner < subs), end + sizes_ref[jnp.minimum(owner, subs - 1)], end)
            live = owner < subs
            here = slice(j * BLOCK, (j + 1) * BLOCK)
            coupling = lax.dot_general(blk_ref[inc_ref[tile]], phi_ref[j], contract, preferred_element_type=F32)
            response = diag_ref[j : j + 1, :] * loads_ref[:, here].astype(F32) + coupling
            response = jnp.where(live, response, jnp.zeros_like(response))
            adj_ref[:, here] = response.astype(BF16)
            total = jnp.sum(response * state_ref[:, here].astype(F32), axis=1, keepdims=True)
            sens = sens + jnp.where(lane == owner, total, jnp.zeros_like(sens))
        sens_ref[...] = jnp.where(step == steps - 1, sens * sens_scale, sens)
        at_ref[0] = owner
        at_ref[1] = end

    return pl.pallas_call(
        kernel,
        out_shape=(
            jax.ShapeDtypeStruct(loads.shape, BF16),
            jax.ShapeDtypeStruct((load_cols, subs), F32),
        ),
        grid_spec=pltpu.PrefetchScalarGridSpec(
            num_scalar_prefetch=2,
            grid=(steps,),
            in_specs=[
                pl.BlockSpec(amp.shape, lambda i, *_: (0, 0, 0)),
                pl.BlockSpec((load_cols, per_step * BLOCK), lambda i, *_: (0, i)),
                pl.BlockSpec((load_cols, per_step * BLOCK), lambda i, *_: (0, i)),
                pl.BlockSpec((per_step, BLOCK), lambda i, *_: (i, 0)),
                pl.BlockSpec((per_step, BLOCK, BLOCK), lambda i, *_: (i, 0, 0)),
            ],
            out_specs=(
                pl.BlockSpec((load_cols, per_step * BLOCK), lambda i, *_: (0, i)),
                pl.BlockSpec((load_cols, subs), lambda i, *_: (0, 0)),
            ),
            scratch_shapes=[
                pltpu.VMEM((blocks, load_cols, BLOCK), BF16),
                pltpu.SMEM((2,), jnp.int32),
            ],
        ),
        compiler_params=pltpu.CompilerParams(vmem_limit_bytes=40 << 20),
        name="recover",
    )(inc, sizes, amp, loads, state, diag, phi)


def exchange(parts, axis):
    return lax.all_to_all(parts, axis, 0, 0, tiled=True)


def total_of(parts):
    return jnp.sum(parts.astype(F32), axis=0).astype(BF16)


def to_all(shard, peers):
    return jnp.broadcast_to(shard[None], (peers, *shard.shape))


def body(loads, state, modal_diag, phi, incidence, sizes, factor):
    load_cols = loads.shape[0]
    wide = lax.axis_size(WIDE)
    deep = lax.axis_size("z")
    frows = factor.shape[0]
    partial, own = condense(incidence, sizes, loads, phi, factor, wide, 8)
    other = lax.ppermute(own, "c", [(0, 1), (1, 0)])
    own_loads = total_of(exchange(partial, WIDE))
    chip_loads = exchange(to_all(own_loads, deep), "z").reshape(deep * load_cols, frows)
    rows = deep * load_cols
    image_part = times_factor(chip_loads, own, other, 4)
    image_part = total_of(exchange(image_part.reshape(wide, rows // wide, -1), WIDE))
    image = exchange(to_all(image_part, wide), WIDE).reshape(rows, -1)
    amp_part = times_transpose(image, own, other, 8)
    amp = total_of(exchange(amp_part.reshape(deep, load_cols, frows), "z"))
    amp_all = exchange(to_all(amp, wide), WIDE)
    diag = modal_diag.reshape(-1, BLOCK)
    return recover(incidence, sizes, amp_all, loads, state, diag, phi, 8)


def solution(mesh):
    fine = Mesh(mesh.devices.reshape(4, 4, 4, 2), ("x", "y", "z", "c"))
    wide, narrow = WIDE, ("z", "c")
    return jax.shard_map(
        body,
        mesh=fine,
        in_specs=(
            P(narrow, wide),
            P(narrow, wide),
            P(wide),
            P(wide, None, None),
            P(wide),
            P(wide),
            P(wide, narrow),
        ),
        out_specs=(P(narrow, wide), P(narrow, wide)),
        check_vma=False,
    )
```

```python
import jax
import jax.numpy as jnp
from jax import lax
from jax.experimental import pallas as pl
from jax.experimental.pallas import tpu as pltpu
from jax.sharding import Mesh, PartitionSpec as P

sens_scale = 0.0625
BLOCK = 128
WIDE = ("x", "y")
F32, BF16 = jnp.float32, jnp.bfloat16
OUTSIDE = pl.BlockSpec(memory_space=pltpu.HBM)
INSIDE = pl.BlockSpec(memory_space=pltpu.VMEM)
PAIR = 2 * BLOCK


def outside(array):
    return pltpu.with_memory_space_constraint(array, pltpu.HBM)


def room(mib):
    return pltpu.CompilerParams(vmem_limit_bytes=mib << 20)


def condense(inc, sizes, loads, phi, factor, peers, chunks, unroll):
    load_cols = loads.shape[0]
    tiles = phi.shape[0]
    subs = sizes.shape[0]
    frows, fcols = factor.shape
    per = frows // BLOCK
    blocks = peers * per
    some = tiles // chunks
    fsome = frows // chunks

    def kernel(inc_hbm, sizes_hbm, loads_hbm, phi_hbm, f_hbm, out_ref, loads_ref, phi_ref, own_ref, *scratch):
        acc_ref, f_ref, inc_ref, sizes_ref, loads_sem, phi_sem, f_sem, scalar_sem = scratch

        def loads_copy(c):
            cols = pl.ds(c * some * BLOCK, some * BLOCK)
            return pltpu.make_async_copy(loads_hbm.at[:, cols], loads_ref.at[:, cols], loads_sem.at[c])

        def phi_copy(c):
            rows = pl.ds(c * some, some)
            return pltpu.make_async_copy(phi_hbm.at[rows], phi_ref.at[rows], phi_sem.at[c])

        def f_copy(c):
            rows = pl.ds(c * fsome, fsome)
            return pltpu.make_async_copy(f_hbm.at[rows], f_ref.at[rows], f_sem.at[c])

        inc_copy = pltpu.make_async_copy(inc_hbm, inc_ref, scalar_sem.at[0])
        sizes_copy = pltpu.make_async_copy(sizes_hbm, sizes_ref, scalar_sem.at[1])
        sizes_copy.start()
        inc_copy.start()
        for c in range(chunks):
            loads_copy(c).start()
            phi_copy(c).start()
            f_copy(c).start()
        acc_ref[...] = jnp.zeros_like(acc_ref)
        sizes_copy.wait()
        live = lax.fori_loop(0, subs, lambda s, n: n + sizes_ref[s], jnp.int32(0), unroll=16)
        inc_copy.wait()

        def part(p, carry):
            for j in range(0, unroll, 2):
                tile = p * unroll + j
                if j % some == 0:
                    c = p * (unroll // some) + j // some
                    loads_copy(c).wait()
                    phi_copy(c).wait()
                cols = pl.multiple_of(tile * BLOCK, PAIR)
                rows = jnp.concatenate([loads_ref[:, pl.ds(cols, BLOCK)], loads_ref[:, pl.ds(cols + BLOCK, BLOCK)]], axis=0)
                both = jnp.concatenate([phi_ref[tile], phi_ref[tile + 1]], axis=1)
                terms = jnp.dot(rows, both, preferred_element_type=F32)
                first, second = terms[:load_cols, :BLOCK], terms[load_cols:, BLOCK:]
                acc_ref[inc_ref[tile]] += jnp.where(tile < live, first, jnp.zeros_like(first))
                acc_ref[inc_ref[tile + 1]] += jnp.where(tile + 1 < live, second, jnp.zeros_like(second))
            for i in range(unroll // some):
                c = p * (unroll // some) + i
                f_copy(c).wait()
                rows = pl.ds(c * fsome, fsome)
                own_ref[rows] = f_ref[rows].astype(BF16)
            return carry

        lax.fori_loop(0, tiles // unroll, part, 0)
        for b in range(blocks):
            out_ref[b // per, :, (b % per) * BLOCK : (b % per + 1) * BLOCK] = acc_ref[b].astype(BF16)

    return pl.pallas_call(
        kernel,
        out_shape=(
            jax.ShapeDtypeStruct((peers, load_cols, frows), BF16),
            pltpu.VMEM(loads.shape, BF16),
            pltpu.VMEM(phi.shape, BF16),
            pltpu.VMEM(factor.shape, BF16),
        ),
        in_specs=[OUTSIDE] * 5,
        out_specs=(INSIDE,) * 4,
        scratch_shapes=[
            pltpu.VMEM((blocks, load_cols, BLOCK), F32),
            pltpu.VMEM(factor.shape, F32),
            pltpu.SMEM(inc.shape, jnp.int32),
            pltpu.SMEM(sizes.shape, jnp.int32),
            pltpu.SemaphoreType.DMA((chunks,)),
            pltpu.SemaphoreType.DMA((chunks,)),
            pltpu.SemaphoreType.DMA((chunks,)),
            pltpu.SemaphoreType.DMA((2,)),
        ],
        compiler_params=room(12),
        name="condense",
    )(*[outside(a) for a in (inc, sizes, loads, phi, factor)])


def total_of(parts, copies):
    shape = parts[0].shape[1:] if len(parts) == 1 else parts[0].shape

    def kernel(*refs):
        *part_refs, out_ref = refs
        if len(parts) == 1:
            terms = [part_refs[0][i] for i in range(parts[0].shape[0])]
        else:
            terms = [r[...] for r in part_refs]
        total = terms[0].astype(F32)
        for term in terms[1:]:
            total += term.astype(F32)
        total = total.astype(BF16)
        if copies:
            for i in range(copies):
                out_ref[i] = total
        else:
            out_ref[...] = total

    return pl.pallas_call(
        kernel,
        out_shape=jax.ShapeDtypeStruct((copies, *shape) if copies else shape, BF16),
        in_specs=[INSIDE] * len(parts),
        out_specs=INSIDE,
        compiler_params=room(4),
        name="total_of",
    )(*parts)


def times_factor(parts, own, other, width):
    rows = len(parts) * parts[0].shape[0]
    cols = own.shape[1]

    def kernel(*refs):
        *part_refs, own_ref, other_ref, out_ref = refs
        left = jnp.concatenate([r[...] for r in part_refs], axis=0)
        for at, half_ref in ((0, own_ref), (cols, other_ref)):
            for c in range(0, cols, width):
                product = jnp.dot(left, half_ref[:, c : c + width], preferred_element_type=F32)
                out_ref[:, at + c : at + c + width] = product.astype(BF16)

    return pl.pallas_call(
        kernel,
        out_shape=jax.ShapeDtypeStruct((rows, 2 * cols), BF16),
        in_specs=[INSIDE] * (len(parts) + 2),
        out_specs=INSIDE,
        compiler_params=room(8),
        name="times_factor",
    )(*parts, own, other)


def times_transpose(image, own, other, groups, height):
    rows = image.shape[0]
    frows, cols = own.shape
    group = rows // groups
    contract = (((1,), (1,)), ((), ()))

    def kernel(image_ref, own_ref, other_ref, *outs):
        for c in range(frows // height):
            some = slice(c * height, (c + 1) * height)
            total = lax.dot_general(image_ref[:, :cols], own_ref[some], contract, preferred_element_type=F32)
            total += lax.dot_general(image_ref[:, cols:], other_ref[some], contract, preferred_element_type=F32)
            for g in range(groups):
                outs[g][:, some] = total[g * group : (g + 1) * group].astype(BF16)

    return pl.pallas_call(
        kernel,
        out_shape=[jax.ShapeDtypeStruct((group, frows), BF16)] * groups,
        in_specs=[INSIDE] * 3,
        out_specs=[INSIDE] * groups,
        compiler_params=room(8),
        name="times_transpose",
    )(image, own, other)


def recover(inc, sizes, amp, loads, state, diag, phi, unroll):
    load_cols = loads.shape[0]
    tiles = phi.shape[0]
    subs = sizes.shape[0]
    peers, _, frows = amp.shape
    per = frows // BLOCK
    blocks = peers * per
    parts = tiles // unroll
    contract = (((1,), (1,)), ((), ()))

    def kernel(inc_hbm, sizes_hbm, amp_ref, loads_ref, state_ref, diag_ref, phi_ref, adj_hbm, sens_ref, *scratch):
        adj_ref, blk_ref, inc_ref, sizes_ref, sem, scalar_sem = scratch
        inc_copy = pltpu.make_async_copy(inc_hbm, inc_ref, scalar_sem.at[0])
        sizes_copy = pltpu.make_async_copy(sizes_hbm, sizes_ref, scalar_sem.at[1])
        inc_copy.start()
        sizes_copy.start()
        for b in range(blocks):
            blk_ref[b] = amp_ref[b // per, :, (b % per) * BLOCK : (b % per + 1) * BLOCK]
        lane = lax.broadcasted_iota(jnp.int32, (load_cols, subs), 1)
        inc_copy.wait()
        sizes_copy.wait()

        def adj_copy(p):
            cols = pl.ds(pl.multiple_of(p * unroll * BLOCK, BLOCK), unroll * BLOCK)
            return pltpu.make_async_copy(adj_ref.at[:, cols], adj_hbm.at[:, cols], sem.at[p])

        def part(p, carry):
            owner, end, sens = carry
            for j in range(0, unroll, 2):
                tile = p * unroll + j
                rows = jnp.concatenate([blk_ref[inc_ref[tile]], blk_ref[inc_ref[tile + 1]]], axis=0)
                both = phi_ref[pl.ds(tile, 2)].reshape(PAIR, BLOCK)
                product = lax.dot_general(rows, both, contract, preferred_element_type=F32)
                couplings = (product[:load_cols, :BLOCK], product[load_cols:, BLOCK:])
                for q, coupling in enumerate(couplings):
                    past = (tile + q >= end) & (owner < subs)
                    owner = jnp.where(past, owner + 1, owner)
                    end = jnp.where(past & (owner < subs), end + sizes_ref[jnp.minimum(owner, subs - 1)], end)
                    cols = pl.ds(pl.multiple_of((tile + q) * BLOCK, BLOCK), BLOCK)
                    response = diag_ref[pl.ds(tile + q, 1), :] * loads_ref[:, cols].astype(F32) + coupling
                    response = jnp.where(owner < subs, response, jnp.zeros_like(response))
                    adj_ref[:, cols] = response.astype(BF16)
                    total = jnp.sum(response * state_ref[:, cols].astype(F32), axis=1, keepdims=True)
                    sens = sens + jnp.where(lane == owner, total, jnp.zeros_like(sens))
            adj_copy(p).start()
            return owner, end, sens

        start = (jnp.int32(0), sizes_ref[0], jnp.zeros((load_cols, subs), F32))
        _, _, sens = lax.fori_loop(0, parts, part, start)
        sens_ref[...] = sens * sens_scale
        for p in range(parts):
            adj_copy(p).wait()

    return pl.pallas_call(
        kernel,
        out_shape=(
            jax.ShapeDtypeStruct(loads.shape, BF16),
            jax.ShapeDtypeStruct((load_cols, subs), F32),
        ),
        in_specs=[OUTSIDE] * 2 + [INSIDE] * 5,
        out_specs=(OUTSIDE, INSIDE),
        scratch_shapes=[
            pltpu.VMEM(loads.shape, BF16),
            pltpu.VMEM((blocks, load_cols, BLOCK), BF16),
            pltpu.SMEM(inc.shape, jnp.int32),
            pltpu.SMEM(sizes.shape, jnp.int32),
            pltpu.SemaphoreType.DMA((parts,)),
            pltpu.SemaphoreType.DMA((2,)),
        ],
        compiler_params=room(6),
        name="recover",
    )(inc, sizes, amp, loads, state, diag, phi)


def exchange(parts, axis):
    return lax.all_to_all(parts, axis, 0, 0, tiled=True)


def moved(value, axis, by):
    peers = lax.axis_size(axis)
    return lax.ppermute(value, axis, [(i, (i + by) % peers) for i in range(peers)])


def body(loads, state, modal_diag, phi, incidence, sizes, factor):
    wide = lax.axis_size(WIDE)
    frows = factor.shape[0]
    shifts = (1, 3, 2)
    partial, loads_in, phi_in, own = condense(incidence, sizes, loads, phi, factor, wide, 8, 64)
    other = moved(own, "c", 1)
    own_loads = total_of([exchange(partial, WIDE)], 0)
    chip_loads = [own_loads] + [moved(own_loads, "z", s) for s in shifts]
    image_part = times_factor(chip_loads, own, other, 512)
    rows = image_part.shape[0]
    image_parts = exchange(image_part.reshape(wide, rows // wide, -1), WIDE)
    image = exchange(total_of([image_parts], wide), WIDE).reshape(rows, -1)
    diag = modal_diag.reshape(-1, BLOCK)
    amp_parts = times_transpose(image, own, other, 4, 128)
    amp_parts = [amp_parts[0]] + [moved(a, "z", -s) for a, s in zip(amp_parts[1:], shifts)]
    amp_all = exchange(total_of(amp_parts, wide), WIDE)
    return recover(incidence, sizes, amp_all, loads_in, state, diag, phi_in, 64)


def solution(mesh):
    fine = Mesh(mesh.devices.reshape(4, 4, 4, 2), ("x", "y", "z", "c"))
    wide, narrow = WIDE, ("z", "c")
    return jax.shard_map(
        body,
        mesh=fine,
        in_specs=(
            P(narrow, wide),
            P(narrow, wide),
            P(wide),
            P(wide, None, None),
            P(wide),
            P(wide),
            P(wide, narrow),
        ),
        out_specs=(P(narrow, wide), P(narrow, wide)),
        check_vma=False,
    )
```

```python
import jax
import jax.numpy as jnp
from jax import lax
from jax.experimental import pallas as pl
from jax.experimental.pallas import tpu as pltpu
from jax.sharding import Mesh, PartitionSpec as P

sens_scale = 0.0625
BLOCK = 128
WIDE = ("x", "y")
F32, BF16 = jnp.float32, jnp.bfloat16
OUTSIDE = pl.BlockSpec(memory_space=pltpu.HBM)
INSIDE = pl.BlockSpec(memory_space=pltpu.VMEM)
PAIR = 2 * BLOCK


def outside(array):
    return pltpu.with_memory_space_constraint(array, pltpu.HBM)


def room(mib):
    return pltpu.CompilerParams(vmem_limit_bytes=mib << 20)


def condense(inc, sizes, loads, phi, peers, frows, chunks, unroll):
    load_cols = loads.shape[0]
    tiles = phi.shape[0]
    subs = sizes.shape[0]
    per = frows // BLOCK
    blocks = peers * per
    some = tiles // chunks

    def kernel(inc_hbm, sizes_hbm, loads_hbm, phi_hbm, out_ref, loads_ref, phi_ref, *scratch):
        acc_ref, inc_ref, sizes_ref, loads_sem, phi_sem, scalar_sem = scratch

        def loads_copy(c):
            cols = pl.ds(c * some * BLOCK, some * BLOCK)
            return pltpu.make_async_copy(loads_hbm.at[:, cols], loads_ref.at[:, cols], loads_sem.at[c])

        def phi_copy(c):
            rows = pl.ds(c * some, some)
            return pltpu.make_async_copy(phi_hbm.at[rows], phi_ref.at[rows], phi_sem.at[c])

        inc_copy = pltpu.make_async_copy(inc_hbm, inc_ref, scalar_sem.at[0])
        sizes_copy = pltpu.make_async_copy(sizes_hbm, sizes_ref, scalar_sem.at[1])
        sizes_copy.start()
        inc_copy.start()
        for c in range(chunks):
            loads_copy(c).start()
            phi_copy(c).start()
        acc_ref[...] = jnp.zeros_like(acc_ref)
        sizes_copy.wait()
        live = lax.fori_loop(0, subs, lambda s, n: n + sizes_ref[s], jnp.int32(0), unroll=16)
        inc_copy.wait()

        def part(p, carry):
            for j in range(0, unroll, 2):
                tile = p * unroll + j
                if j % some == 0:
                    c = p * (unroll // some) + j // some
                    loads_copy(c).wait()
                    phi_copy(c).wait()
                cols = pl.multiple_of(tile * BLOCK, PAIR)
                rows = jnp.concatenate([loads_ref[:, pl.ds(cols, BLOCK)], loads_ref[:, pl.ds(cols + BLOCK, BLOCK)]], axis=0)
                both = jnp.concatenate([phi_ref[tile], phi_ref[tile + 1]], axis=1)
                terms = jnp.dot(rows, both, preferred_element_type=F32)
                first, second = terms[:load_cols, :BLOCK], terms[load_cols:, BLOCK:]
                acc_ref[inc_ref[tile]] += jnp.where(tile < live, first, jnp.zeros_like(first))
                acc_ref[inc_ref[tile + 1]] += jnp.where(tile + 1 < live, second, jnp.zeros_like(second))
            return carry

        lax.fori_loop(0, tiles // unroll, part, 0)
        for b in range(blocks):
            out_ref[b // per, :, (b % per) * BLOCK : (b % per + 1) * BLOCK] = acc_ref[b].astype(BF16)

    return pl.pallas_call(
        kernel,
        out_shape=(
            jax.ShapeDtypeStruct((peers, load_cols, frows), BF16),
            pltpu.VMEM(loads.shape, BF16),
            pltpu.VMEM(phi.shape, BF16),
        ),
        in_specs=[OUTSIDE] * 4,
        out_specs=(INSIDE,) * 3,
        scratch_shapes=[
            pltpu.VMEM((blocks, load_cols, BLOCK), F32),
            pltpu.SMEM(inc.shape, jnp.int32),
            pltpu.SMEM(sizes.shape, jnp.int32),
            pltpu.SemaphoreType.DMA((chunks,)),
            pltpu.SemaphoreType.DMA((chunks,)),
            pltpu.SemaphoreType.DMA((2,)),
        ],
        compiler_params=room(4),
        name="condense",
    )(*[outside(a) for a in (inc, sizes, loads, phi)])


def rounded(own, other, after):
    def kernel(own_ref, other_ref, after_ref, own_out, other_out):
        own_out[...] = own_ref[...].astype(BF16)
        other_out[...] = other_ref[...].astype(BF16)

    return pl.pallas_call(
        kernel,
        out_shape=(pltpu.VMEM(own.shape, BF16), pltpu.VMEM(own.shape, BF16)),
        in_specs=[INSIDE] * 3,
        out_specs=(INSIDE, INSIDE),
        compiler_params=room(4),
        cost_estimate=pl.CostEstimate(flops=2 * own.size, transcendentals=0, bytes_accessed=12 * own.size),
        name="rounded",
    )(own, other, after)


def total_of(parts, copies):
    shape = parts[0].shape[1:] if len(parts) == 1 else parts[0].shape

    def kernel(*refs):
        *part_refs, out_ref = refs
        if len(parts) == 1:
            terms = [part_refs[0][i] for i in range(parts[0].shape[0])]
        else:
            terms = [r[...] for r in part_refs]
        total = terms[0].astype(F32)
        for term in terms[1:]:
            total += term.astype(F32)
        total = total.astype(BF16)
        if copies:
            for i in range(copies):
                out_ref[i] = total
        else:
            out_ref[...] = total

    return pl.pallas_call(
        kernel,
        out_shape=jax.ShapeDtypeStruct((copies, *shape) if copies else shape, BF16),
        in_specs=[INSIDE] * len(parts),
        out_specs=INSIDE,
        compiler_params=room(4),
        name="total_of",
    )(*parts)


def times_factor(parts, own, other, width):
    rows = len(parts) * parts[0].shape[0]
    cols = own.shape[1]

    def kernel(*refs):
        *part_refs, own_ref, other_ref, out_ref = refs
        left = jnp.concatenate([r[...] for r in part_refs], axis=0)
        for at, half_ref in ((0, own_ref), (cols, other_ref)):
            for c in range(0, cols, width):
                product = jnp.dot(left, half_ref[:, c : c + width], preferred_element_type=F32)
                out_ref[:, at + c : at + c + width] = product.astype(BF16)

    return pl.pallas_call(
        kernel,
        out_shape=jax.ShapeDtypeStruct((rows, 2 * cols), BF16),
        in_specs=[INSIDE] * (len(parts) + 2),
        out_specs=INSIDE,
        compiler_params=room(8),
        name="times_factor",
    )(*parts, own, other)


def times_transpose(image, own, other, groups, height):
    rows = image.shape[0]
    frows, cols = own.shape
    group = rows // groups
    contract = (((1,), (1,)), ((), ()))

    def kernel(image_ref, own_ref, other_ref, *outs):
        for c in range(frows // height):
            some = slice(c * height, (c + 1) * height)
            total = lax.dot_general(image_ref[:, :cols], own_ref[some], contract, preferred_element_type=F32)
            total += lax.dot_general(image_ref[:, cols:], other_ref[some], contract, preferred_element_type=F32)
            for g in range(groups):
                outs[g][:, some] = total[g * group : (g + 1) * group].astype(BF16)

    return pl.pallas_call(
        kernel,
        out_shape=[jax.ShapeDtypeStruct((group, frows), BF16)] * groups,
        in_specs=[INSIDE] * 3,
        out_specs=[INSIDE] * groups,
        compiler_params=room(8),
        name="times_transpose",
    )(image, own, other)


def recover(inc, sizes, amp, loads, state, diag, phi, unroll, some):
    load_cols = loads.shape[0]
    tiles = phi.shape[0]
    subs = sizes.shape[0]
    per = amp.shape[2] // BLOCK
    blocks = amp.shape[0] * per
    parts = tiles // unroll
    pieces = tiles // some
    contract = (((1,), (1,)), ((), ()))

    def kernel(inc_hbm, sizes_hbm, amp_ref, loads_ref, state_ref, diag_ref, phi_ref, adj_hbm, sens_ref, *scratch):
        adj_ref, blk_ref, inc_ref, sizes_ref, sem, scalar_sem = scratch
        inc_copy = pltpu.make_async_copy(inc_hbm, inc_ref, scalar_sem.at[0])
        sizes_copy = pltpu.make_async_copy(sizes_hbm, sizes_ref, scalar_sem.at[1])
        inc_copy.start()
        sizes_copy.start()
        for b in range(blocks):
            blk_ref[b] = amp_ref[b // per, :, (b % per) * BLOCK : (b % per + 1) * BLOCK]
        lane = lax.broadcasted_iota(jnp.int32, (load_cols, subs), 1)
        inc_copy.wait()
        sizes_copy.wait()

        def adj_copy(p):
            cols = pl.ds(pl.multiple_of(p * some * BLOCK, BLOCK), some * BLOCK)
            return pltpu.make_async_copy(adj_ref.at[:, cols], adj_hbm.at[:, cols], sem.at[p])

        def part(p, carry):
            owner, end, sens = carry
            for j in range(0, unroll, 2):
                tile = p * unroll + j
                rows = jnp.concatenate([blk_ref[inc_ref[tile]], blk_ref[inc_ref[tile + 1]]], axis=0)
                both = phi_ref[pl.ds(tile, 2)].reshape(PAIR, BLOCK)
                product = lax.dot_general(rows, both, contract, preferred_element_type=F32)
                couplings = (product[:load_cols, :BLOCK], product[load_cols:, BLOCK:])
                for q, coupling in enumerate(couplings):
                    past = (tile + q >= end) & (owner < subs)
                    owner = jnp.where(past, owner + 1, owner)
                    end = jnp.where(past & (owner < subs), end + sizes_ref[jnp.minimum(owner, subs - 1)], end)
                    cols = pl.ds(pl.multiple_of((tile + q) * BLOCK, BLOCK), BLOCK)
                    response = diag_ref[pl.ds(tile + q, 1), :] * loads_ref[:, cols].astype(F32) + coupling
                    response = jnp.where(owner < subs, response, jnp.zeros_like(response))
                    adj_ref[:, cols] = response.astype(BF16)
                    total = jnp.sum(response * state_ref[:, cols].astype(F32), axis=1, keepdims=True)
                    sens = sens + jnp.where(lane == owner, total, jnp.zeros_like(sens))
                if (j + 2) % some == 0:
                    adj_copy(p * (unroll // some) + j // some).start()
            return owner, end, sens

        start = (jnp.int32(0), sizes_ref[0], jnp.zeros((load_cols, subs), F32))
        _, _, sens = lax.fori_loop(0, parts, part, start)
        sens_ref[...] = sens * sens_scale
        for p in range(pieces):
            adj_copy(p).wait()

    return pl.pallas_call(
        kernel,
        out_shape=(
            jax.ShapeDtypeStruct(loads.shape, BF16),
            jax.ShapeDtypeStruct((load_cols, subs), F32),
        ),
        in_specs=[OUTSIDE] * 2 + [INSIDE] * 5,
        out_specs=(OUTSIDE, INSIDE),
        scratch_shapes=[
            pltpu.VMEM(loads.shape, BF16),
            pltpu.VMEM((blocks, load_cols, BLOCK), BF16),
            pltpu.SMEM(inc.shape, jnp.int32),
            pltpu.SMEM(sizes.shape, jnp.int32),
            pltpu.SemaphoreType.DMA((pieces,)),
            pltpu.SemaphoreType.DMA((2,)),
        ],
        compiler_params=room(6),
        name="recover",
    )(inc, sizes, amp, loads, state, diag, phi)


def exchange(parts, axis):
    return lax.all_to_all(parts, axis, 0, 0, tiled=True)


def moved(value, axis, by):
    peers = lax.axis_size(axis)
    return lax.ppermute(value, axis, [(i, (i + by) % peers) for i in range(peers)])


def body(loads, state, modal_diag, phi, incidence, sizes, factor):
    wide = lax.axis_size(WIDE)
    frows = factor.shape[0]
    shifts = (1, 3, 2)
    partial, loads_in, phi_in = condense(incidence, sizes, loads, phi, wide, factor.shape[0], 8, 128)
    other = moved(factor, "c", 1)
    own_loads = total_of([exchange(partial, WIDE)], 0)
    own, other = rounded(factor, other, own_loads)
    chip_loads = [own_loads] + [moved(own_loads, "z", s) for s in shifts]
    image_part = times_factor(chip_loads, own, other, 512)
    rows = image_part.shape[0]
    image_parts = exchange(image_part.reshape(wide, rows // wide, -1), WIDE)
    image = exchange(total_of([image_parts], wide), WIDE).reshape(rows, -1)
    diag = modal_diag.reshape(-1, BLOCK)
    amp_parts = times_transpose(image, own, other, 4, 128)
    amp_parts = [amp_parts[0]] + [moved(a, "z", -s) for a, s in zip(amp_parts[1:], shifts)]
    amp_all = exchange(total_of(amp_parts, wide), WIDE)
    return recover(incidence, sizes, amp_all, loads_in, state, diag, phi_in, 128, 32)


def solution(mesh):
    fine = Mesh(mesh.devices.reshape(4, 4, 4, 2), ("x", "y", "z", "c"))
    wide, narrow = WIDE, ("z", "c")
    return jax.shard_map(
        body,
        mesh=fine,
        in_specs=(
            P(narrow, wide),
            P(narrow, wide),
            P(wide),
            P(wide, None, None),
            P(wide),
            P(wide),
            P(wide, narrow),
        ),
        out_specs=(P(narrow, wide), P(narrow, wide)),
        check_vma=False,
    )
```

```python
import jax
import jax.numpy as jnp
from jax import lax
from jax.experimental import pallas as pl
from jax.experimental.pallas import tpu as pltpu
from jax.sharding import Mesh, PartitionSpec as P

sens_scale = 0.0625
BLOCK = 128
WIDE = ("x", "y")
F32, BF16 = jnp.float32, jnp.bfloat16
OUTSIDE = pl.BlockSpec(memory_space=pltpu.HBM)
INSIDE = pl.BlockSpec(memory_space=pltpu.VMEM)
PAIR = 2 * BLOCK


def outside(array):
    return pltpu.with_memory_space_constraint(array, pltpu.HBM)


def room(mib):
    return pltpu.CompilerParams(vmem_limit_bytes=mib << 20)


def condense(inc, sizes, loads, phi, peers, frows, chunks, unroll):
    load_cols = loads.shape[0]
    tiles = phi.shape[0]
    subs = sizes.shape[0]
    per = frows // BLOCK
    blocks = peers * per
    some = tiles // chunks

    def kernel(inc_hbm, sizes_hbm, loads_hbm, phi_hbm, out_ref, loads_ref, phi_ref, *scratch):
        acc_ref, inc_ref, sizes_ref, loads_sem, phi_sem, scalar_sem = scratch

        def loads_copy(c):
            cols = pl.ds(c * some * BLOCK, some * BLOCK)
            return pltpu.make_async_copy(loads_hbm.at[:, cols], loads_ref.at[:, cols], loads_sem.at[c])

        def phi_copy(c):
            rows = pl.ds(c * some, some)
            return pltpu.make_async_copy(phi_hbm.at[rows], phi_ref.at[rows], phi_sem.at[c])

        inc_copy = pltpu.make_async_copy(inc_hbm, inc_ref, scalar_sem.at[0])
        sizes_copy = pltpu.make_async_copy(sizes_hbm, sizes_ref, scalar_sem.at[1])
        sizes_copy.start()
        inc_copy.start()
        for c in range(chunks):
            loads_copy(c).start()
            phi_copy(c).start()
        acc_ref[...] = jnp.zeros_like(acc_ref)
        sizes_copy.wait()
        live = lax.fori_loop(0, subs, lambda s, n: n + sizes_ref[s], jnp.int32(0), unroll=16)
        inc_copy.wait()

        def part(p, carry):
            for j in range(0, unroll, 2):
                tile = p * unroll + j
                if j % some == 0:
                    c = p * (unroll // some) + j // some
                    loads_copy(c).wait()
                    phi_copy(c).wait()
                cols = pl.multiple_of(tile * BLOCK, PAIR)
                rows = jnp.concatenate([loads_ref[:, pl.ds(cols, BLOCK)], loads_ref[:, pl.ds(cols + BLOCK, BLOCK)]], axis=0)
                both = jnp.concatenate([phi_ref[tile], phi_ref[tile + 1]], axis=1)
                terms = jnp.dot(rows, both, preferred_element_type=F32)
                first, second = terms[:load_cols, :BLOCK], terms[load_cols:, BLOCK:]
                acc_ref[inc_ref[tile]] += jnp.where(tile < live, first, jnp.zeros_like(first))
                acc_ref[inc_ref[tile + 1]] += jnp.where(tile + 1 < live, second, jnp.zeros_like(second))
            return carry

        lax.fori_loop(0, tiles // unroll, part, 0)
        for b in range(blocks):
            out_ref[b // per, :, (b % per) * BLOCK : (b % per + 1) * BLOCK] = acc_ref[b].astype(BF16)

    return pl.pallas_call(
        kernel,
        out_shape=(
            jax.ShapeDtypeStruct((peers, load_cols, frows), BF16),
            pltpu.VMEM(loads.shape, BF16),
            pltpu.VMEM(phi.shape, BF16),
        ),
        in_specs=[OUTSIDE] * 4,
        out_specs=(INSIDE,) * 3,
        scratch_shapes=[
            pltpu.VMEM((blocks, load_cols, BLOCK), F32),
            pltpu.SMEM(inc.shape, jnp.int32),
            pltpu.SMEM(sizes.shape, jnp.int32),
            pltpu.SemaphoreType.DMA((chunks,)),
            pltpu.SemaphoreType.DMA((chunks,)),
            pltpu.SemaphoreType.DMA((2,)),
        ],
        compiler_params=room(4),
        name="condense",
    )(*[outside(a) for a in (inc, sizes, loads, phi)])


def rounded(own, other, after):
    def kernel(own_ref, other_ref, after_ref, own_out, other_out):
        own_out[...] = own_ref[...].astype(BF16)
        other_out[...] = other_ref[...].astype(BF16)

    return pl.pallas_call(
        kernel,
        out_shape=(pltpu.VMEM(own.shape, BF16), pltpu.VMEM(own.shape, BF16)),
        in_specs=[INSIDE] * 3,
        out_specs=(INSIDE, INSIDE),
        compiler_params=room(4),
        cost_estimate=pl.CostEstimate(flops=2 * own.size, transcendentals=0, bytes_accessed=12 * own.size),
        name="rounded",
    )(own, other, after)


def total_of(parts, copies):
    shape = parts[0].shape[1:] if len(parts) == 1 else parts[0].shape

    def kernel(*refs):
        *part_refs, out_ref = refs
        if len(parts) == 1:
            terms = [part_refs[0][i] for i in range(parts[0].shape[0])]
        else:
            terms = [r[...] for r in part_refs]
        total = terms[0].astype(F32)
        for term in terms[1:]:
            total += term.astype(F32)
        total = total.astype(BF16)
        if copies:
            for i in range(copies):
                out_ref[i] = total
        else:
            out_ref[...] = total

    return pl.pallas_call(
        kernel,
        out_shape=jax.ShapeDtypeStruct((copies, *shape) if copies else shape, BF16),
        in_specs=[INSIDE] * len(parts),
        out_specs=INSIDE,
        compiler_params=room(4),
        name="total_of",
    )(*parts)


def times_factor(parts, own, other, width):
    rows = len(parts) * parts[0].shape[0]
    cols = own.shape[1]

    def kernel(*refs):
        *part_refs, own_ref, other_ref, out_ref = refs
        left = jnp.concatenate([r[...] for r in part_refs], axis=0)
        for at, half_ref in ((0, own_ref), (cols, other_ref)):
            for c in range(0, cols, width):
                product = jnp.dot(left, half_ref[:, c : c + width], preferred_element_type=F32)
                out_ref[:, at + c : at + c + width] = product.astype(BF16)

    return pl.pallas_call(
        kernel,
        out_shape=jax.ShapeDtypeStruct((rows, 2 * cols), BF16),
        in_specs=[INSIDE] * (len(parts) + 2),
        out_specs=INSIDE,
        compiler_params=room(8),
        name="times_factor",
    )(*parts, own, other)


def times_transpose(image, own, other, groups, height):
    rows = image.shape[0]
    frows, cols = own.shape
    group = rows // groups
    contract = (((1,), (1,)), ((), ()))

    def kernel(image_ref, own_ref, other_ref, *outs):
        for c in range(frows // height):
            some = slice(c * height, (c + 1) * height)
            total = lax.dot_general(image_ref[:, :cols], own_ref[some], contract, preferred_element_type=F32)
            total += lax.dot_general(image_ref[:, cols:], other_ref[some], contract, preferred_element_type=F32)
            for g in range(groups):
                outs[g][:, some] = total[g * group : (g + 1) * group].astype(BF16)

    return pl.pallas_call(
        kernel,
        out_shape=[jax.ShapeDtypeStruct((group, frows), BF16)] * groups,
        in_specs=[INSIDE] * 3,
        out_specs=[INSIDE] * groups,
        compiler_params=room(8),
        name="times_transpose",
    )(image, own, other)


def recover(inc, sizes, amp, loads, state, diag, phi, unroll, some):
    load_cols = loads.shape[0]
    tiles = phi.shape[0]
    subs = sizes.shape[0]
    per = amp.shape[2] // BLOCK
    parts = tiles // unroll
    pieces = tiles // some
    contract = (((1,), (1,)), ((), ()))

    def kernel(inc_hbm, sizes_hbm, amp_ref, loads_ref, state_ref, diag_ref, phi_ref, adj_hbm, sens_hbm, *scratch):
        adj_ref, sens_ref, inc_ref, sizes_ref, sem, sens_sem, scalar_sem = scratch
        inc_copy = pltpu.make_async_copy(inc_hbm, inc_ref, scalar_sem.at[0])
        sizes_copy = pltpu.make_async_copy(sizes_hbm, sizes_ref, scalar_sem.at[1])
        inc_copy.start()
        sizes_copy.start()
        lane = lax.broadcasted_iota(jnp.int32, (load_cols, subs), 1)
        inc_copy.wait()
        sizes_copy.wait()

        def block(tile):
            at = inc_ref[tile]
            cols = pl.multiple_of(lax.rem(at, per) * BLOCK, BLOCK)
            return amp_ref[lax.div(at, per), :, pl.ds(cols, BLOCK)]

        def adj_copy(p):
            cols = pl.ds(pl.multiple_of(p * some * BLOCK, BLOCK), some * BLOCK)
            return pltpu.make_async_copy(adj_ref.at[:, cols], adj_hbm.at[:, cols], sem.at[p])

        def part(p, carry):
            owner, end, sens = carry
            for j in range(0, unroll, 2):
                tile = p * unroll + j
                rows = jnp.concatenate([block(tile), block(tile + 1)], axis=0)
                both = phi_ref[pl.ds(tile, 2)].reshape(PAIR, BLOCK)
                product = lax.dot_general(rows, both, contract, preferred_element_type=F32)
                couplings = (product[:load_cols, :BLOCK], product[load_cols:, BLOCK:])
                for q, coupling in enumerate(couplings):
                    past = (tile + q >= end) & (owner < subs)
                    owner = jnp.where(past, owner + 1, owner)
                    end = jnp.where(past & (owner < subs), end + sizes_ref[jnp.minimum(owner, subs - 1)], end)
                    cols = pl.ds(pl.multiple_of((tile + q) * BLOCK, BLOCK), BLOCK)
                    response = diag_ref[pl.ds(tile + q, 1), :] * loads_ref[:, cols].astype(F32) + coupling
                    response = jnp.where(owner < subs, response, jnp.zeros_like(response))
                    adj_ref[:, cols] = response.astype(BF16)
                    total = jnp.sum(response * state_ref[:, cols].astype(F32), axis=1, keepdims=True)
                    sens = sens + jnp.where(lane == owner, total, jnp.zeros_like(sens))
                if (j + 2) % some == 0:
                    adj_copy(p * (unroll // some) + j // some).start()
            return owner, end, sens

        start = (jnp.int32(0), sizes_ref[0], jnp.zeros((load_cols, subs), F32))
        _, _, sens = lax.fori_loop(0, parts, part, start)
        sens_ref[...] = sens * sens_scale
        sens_copy = pltpu.make_async_copy(sens_ref, sens_hbm, sens_sem.at[0])
        sens_copy.start()
        for p in range(pieces):
            adj_copy(p).wait()
        sens_copy.wait()

    return pl.pallas_call(
        kernel,
        out_shape=(
            jax.ShapeDtypeStruct(loads.shape, BF16),
            jax.ShapeDtypeStruct((load_cols, subs), F32),
        ),
        in_specs=[OUTSIDE] * 2 + [INSIDE] * 5,
        out_specs=(OUTSIDE, OUTSIDE),
        scratch_shapes=[
            pltpu.VMEM(loads.shape, BF16),
            pltpu.VMEM((load_cols, subs), F32),
            pltpu.SMEM(inc.shape, jnp.int32),
            pltpu.SMEM(sizes.shape, jnp.int32),
            pltpu.SemaphoreType.DMA((pieces,)),
            pltpu.SemaphoreType.DMA((1,)),
            pltpu.SemaphoreType.DMA((2,)),
        ],
        compiler_params=room(6),
        name="recover",
    )(inc, sizes, amp, loads, state, diag, phi)


def exchange(parts, axis):
    return lax.all_to_all(parts, axis, 0, 0, tiled=True)


def moved(value, axis, by):
    peers = lax.axis_size(axis)
    return lax.ppermute(value, axis, [(i, (i + by) % peers) for i in range(peers)])


def body(loads, state, modal_diag, phi, incidence, sizes, factor):
    wide = lax.axis_size(WIDE)
    frows = factor.shape[0]
    shifts = (1, 3, 2)
    partial, loads_in, phi_in = condense(incidence, sizes, loads, phi, wide, factor.shape[0], 8, 128)
    other = moved(factor, "c", 1)
    own_loads = total_of([exchange(partial, WIDE)], 0)
    own, other = rounded(factor, other, own_loads)
    chip_loads = [own_loads] + [moved(own_loads, "z", s) for s in shifts]
    image_part = times_factor(chip_loads, own, other, 512)
    rows = image_part.shape[0]
    image_parts = exchange(image_part.reshape(wide, rows // wide, -1), WIDE)
    image = exchange(total_of([image_parts], wide), WIDE).reshape(rows, -1)
    diag = modal_diag.reshape(-1, BLOCK)
    amp_parts = times_transpose(image, own, other, 4, 128)
    amp_parts = [amp_parts[0]] + [moved(a, "z", -s) for a, s in zip(amp_parts[1:], shifts)]
    amp_all = exchange(total_of(amp_parts, wide), WIDE)
    return recover(incidence, sizes, amp_all, loads_in, state, diag, phi_in, 256, 32)


def solution(mesh):
    fine = Mesh(mesh.devices.reshape(4, 4, 4, 2), ("x", "y", "z", "c"))
    wide, narrow = WIDE, ("z", "c")
    return jax.shard_map(
        body,
        mesh=fine,
        in_specs=(
            P(narrow, wide),
            P(narrow, wide),
            P(wide),
            P(wide, None, None),
            P(wide),
            P(wide),
            P(wide, narrow),
        ),
        out_specs=(P(narrow, wide), P(narrow, wide)),
        check_vma=False,
    )
```

```python
import jax
import jax.numpy as jnp
from jax import lax
from jax.experimental import pallas as pl
from jax.experimental.pallas import tpu as pltpu
from jax.sharding import Mesh, PartitionSpec as P

sens_scale = 0.0625
BLOCK = 128
WIDE = ("x", "y")
F32, BF16 = jnp.float32, jnp.bfloat16
OUTSIDE = pl.BlockSpec(memory_space=pltpu.HBM)
INSIDE = pl.BlockSpec(memory_space=pltpu.VMEM)
PAIR = 2 * BLOCK


def outside(array):
    return pltpu.with_memory_space_constraint(array, pltpu.HBM)


def room(mib):
    return pltpu.CompilerParams(vmem_limit_bytes=mib << 20)


def condense(inc, sizes, loads, phi, peers, frows, chunks, unroll):
    load_cols = loads.shape[0]
    tiles = phi.shape[0]
    subs = sizes.shape[0]
    per = frows // BLOCK
    blocks = peers * per
    some = tiles // chunks

    def kernel(inc_hbm, sizes_hbm, loads_hbm, phi_hbm, out_ref, loads_ref, phi_ref, *scratch):
        acc_ref, inc_ref, sizes_ref, loads_sem, phi_sem, scalar_sem = scratch

        def loads_copy(c):
            cols = pl.ds(c * some * BLOCK, some * BLOCK)
            return pltpu.make_async_copy(loads_hbm.at[:, cols], loads_ref.at[:, cols], loads_sem.at[c])

        def phi_copy(c):
            rows = pl.ds(c * some, some)
            return pltpu.make_async_copy(phi_hbm.at[rows], phi_ref.at[rows], phi_sem.at[c])

        inc_copy = pltpu.make_async_copy(inc_hbm, inc_ref, scalar_sem.at[0])
        sizes_copy = pltpu.make_async_copy(sizes_hbm, sizes_ref, scalar_sem.at[1])
        sizes_copy.start()
        inc_copy.start()
        for c in range(chunks):
            loads_copy(c).start()
            phi_copy(c).start()
        acc_ref[...] = jnp.zeros_like(acc_ref)
        sizes_copy.wait()
        live = lax.fori_loop(0, subs, lambda s, n: n + sizes_ref[s], jnp.int32(0), unroll=16)
        inc_copy.wait()

        def part(p, carry):
            for j in range(0, unroll, 2):
                tile = p * unroll + j
                if j % some == 0:
                    c = p * (unroll // some) + j // some
                    loads_copy(c).wait()
                    phi_copy(c).wait()
                cols = pl.multiple_of(tile * BLOCK, PAIR)
                rows = jnp.concatenate([loads_ref[:, pl.ds(cols, BLOCK)], loads_ref[:, pl.ds(cols + BLOCK, BLOCK)]], axis=0)
                both = jnp.concatenate([phi_ref[tile], phi_ref[tile + 1]], axis=1)
                terms = jnp.dot(rows, both, preferred_element_type=F32)
                first, second = terms[:load_cols, :BLOCK], terms[load_cols:, BLOCK:]
                acc_ref[inc_ref[tile]] += jnp.where(tile < live, first, jnp.zeros_like(first))
                acc_ref[inc_ref[tile + 1]] += jnp.where(tile + 1 < live, second, jnp.zeros_like(second))
            return carry

        lax.fori_loop(0, tiles // unroll, part, 0)
        for b in range(blocks):
            out_ref[b // per, :, (b % per) * BLOCK : (b % per + 1) * BLOCK] = acc_ref[b].astype(BF16)

    return pl.pallas_call(
        kernel,
        out_shape=(
            jax.ShapeDtypeStruct((peers, load_cols, frows), BF16),
            pltpu.VMEM(loads.shape, BF16),
            pltpu.VMEM(phi.shape, BF16),
        ),
        in_specs=[OUTSIDE] * 4,
        out_specs=(INSIDE,) * 3,
        scratch_shapes=[
            pltpu.VMEM((blocks, load_cols, BLOCK), F32),
            pltpu.SMEM(inc.shape, jnp.int32),
            pltpu.SMEM(sizes.shape, jnp.int32),
            pltpu.SemaphoreType.DMA((chunks,)),
            pltpu.SemaphoreType.DMA((chunks,)),
            pltpu.SemaphoreType.DMA((2,)),
        ],
        compiler_params=room(4),
        name="condense",
    )(*[outside(a) for a in (inc, sizes, loads, phi)])


def rounded(own, other, after):
    def kernel(own_ref, other_ref, after_ref, own_out, other_out):
        own_out[...] = own_ref[...].astype(BF16)
        other_out[...] = other_ref[...].astype(BF16)

    return pl.pallas_call(
        kernel,
        out_shape=(pltpu.VMEM(own.shape, BF16), pltpu.VMEM(own.shape, BF16)),
        in_specs=[INSIDE] * 3,
        out_specs=(INSIDE, INSIDE),
        compiler_params=room(4),
        cost_estimate=pl.CostEstimate(flops=2 * own.size, transcendentals=0, bytes_accessed=12 * own.size),
        name="rounded",
    )(own, other, after)


def total_of(parts, copies):
    shape = parts[0].shape[1:] if len(parts) == 1 else parts[0].shape

    def kernel(*refs):
        *part_refs, out_ref = refs
        if len(parts) == 1:
            terms = [part_refs[0][i] for i in range(parts[0].shape[0])]
        else:
            terms = [r[...] for r in part_refs]
        total = terms[0].astype(F32)
        for term in terms[1:]:
            total += term.astype(F32)
        total = total.astype(BF16)
        if copies:
            for i in range(copies):
                out_ref[i] = total
        else:
            out_ref[...] = total

    return pl.pallas_call(
        kernel,
        out_shape=jax.ShapeDtypeStruct((copies, *shape) if copies else shape, BF16),
        in_specs=[INSIDE] * len(parts),
        out_specs=INSIDE,
        compiler_params=room(4),
        name="total_of",
    )(*parts)


def times_factor(parts, own, other, width):
    rows = len(parts) * parts[0].shape[0]
    cols = own.shape[1]

    def kernel(*refs):
        *part_refs, own_ref, other_ref, out_ref = refs
        left = jnp.concatenate([r[...] for r in part_refs], axis=0)
        for at, half_ref in ((0, own_ref), (cols, other_ref)):
            for c in range(0, cols, width):
                product = jnp.dot(left, half_ref[:, c : c + width], preferred_element_type=F32)
                out_ref[:, at + c : at + c + width] = product.astype(BF16)

    return pl.pallas_call(
        kernel,
        out_shape=jax.ShapeDtypeStruct((rows, 2 * cols), BF16),
        in_specs=[INSIDE] * (len(parts) + 2),
        out_specs=INSIDE,
        compiler_params=room(8),
        name="times_factor",
    )(*parts, own, other)


def times_transpose(image, own, other, groups, height):
    rows = image.shape[0]
    frows, cols = own.shape
    group = rows // groups
    contract = (((1,), (1,)), ((), ()))

    def kernel(image_ref, own_ref, other_ref, *outs):
        for c in range(frows // height):
            some = slice(c * height, (c + 1) * height)
            total = lax.dot_general(image_ref[:, :cols], own_ref[some], contract, preferred_element_type=F32)
            total += lax.dot_general(image_ref[:, cols:], other_ref[some], contract, preferred_element_type=F32)
            for g in range(groups):
                outs[g][:, some] = total[g * group : (g + 1) * group].astype(BF16)

    return pl.pallas_call(
        kernel,
        out_shape=[jax.ShapeDtypeStruct((group, frows), BF16)] * groups,
        in_specs=[INSIDE] * 3,
        out_specs=[INSIDE] * groups,
        compiler_params=room(8),
        name="times_transpose",
    )(image, own, other)


def recover(inc, sizes, amp, loads, state, diag, phi, unroll, some):
    load_cols = loads.shape[0]
    tiles = phi.shape[0]
    subs = sizes.shape[0]
    per = amp.shape[2] // BLOCK
    parts = tiles // unroll
    pieces = tiles // some
    contract = (((1,), (1,)), ((), ()))

    def kernel(inc_hbm, sizes_hbm, amp_ref, loads_ref, state_ref, diag_ref, phi_ref, adj_hbm, sens_hbm, *scratch):
        adj_ref, sens_ref, inc_ref, sizes_ref, sem, sens_sem, scalar_sem = scratch
        inc_copy = pltpu.make_async_copy(inc_hbm, inc_ref, scalar_sem.at[0])
        sizes_copy = pltpu.make_async_copy(sizes_hbm, sizes_ref, scalar_sem.at[1])
        inc_copy.start()
        sizes_copy.start()
        lane = lax.broadcasted_iota(jnp.int32, (load_cols, subs), 1)
        inc_copy.wait()
        sizes_copy.wait()

        def block(tile):
            at = inc_ref[tile]
            cols = pl.multiple_of(lax.rem(at, per) * BLOCK, BLOCK)
            return amp_ref[lax.div(at, per), :, pl.ds(cols, BLOCK)]

        def adj_copy(p):
            cols = pl.ds(pl.multiple_of(p * some * BLOCK, BLOCK), some * BLOCK)
            return pltpu.make_async_copy(adj_ref.at[:, cols], adj_hbm.at[:, cols], sem.at[p])

        def part(p, carry):
            owner, end, sens = carry
            for j in range(0, unroll, 2):
                tile = p * unroll + j
                rows = jnp.concatenate([block(tile), block(tile + 1)], axis=0)
                both = phi_ref[pl.ds(tile, 2)].reshape(PAIR, BLOCK)
                product = lax.dot_general(rows, both, contract, preferred_element_type=F32)
                couplings = (product[:load_cols, :BLOCK], product[load_cols:, BLOCK:])
                for q, coupling in enumerate(couplings):
                    past = (tile + q >= end) & (owner < subs)
                    owner = jnp.where(past, owner + 1, owner)
                    end = jnp.where(past & (owner < subs), end + sizes_ref[jnp.minimum(owner, subs - 1)], end)
                    cols = pl.ds(pl.multiple_of((tile + q) * BLOCK, BLOCK), BLOCK)
                    response = diag_ref[pl.ds(tile + q, 1), :] * loads_ref[:, cols].astype(F32) + coupling
                    response = jnp.where(owner < subs, response, jnp.zeros_like(response))
                    adj_ref[:, cols] = response.astype(BF16)
                    total = jnp.sum(response * state_ref[:, cols].astype(F32), axis=1, keepdims=True)
                    sens = sens + jnp.where(lane == owner, total, jnp.zeros_like(sens))
                if (j + 2) % some == 0:
                    adj_copy(p * (unroll // some) + j // some).start()
            return owner, end, sens

        start = (jnp.int32(0), sizes_ref[0], jnp.zeros((load_cols, subs), F32))
        _, _, sens = lax.fori_loop(0, parts, part, start)
        sens_ref[...] = sens * sens_scale
        sens_copy = pltpu.make_async_copy(sens_ref, sens_hbm, sens_sem.at[0])
        sens_copy.start()
        for p in range(pieces):
            adj_copy(p).wait()
        sens_copy.wait()

    return pl.pallas_call(
        kernel,
        out_shape=(
            jax.ShapeDtypeStruct(loads.shape, BF16),
            jax.ShapeDtypeStruct((load_cols, subs), F32),
        ),
        in_specs=[OUTSIDE] * 2 + [INSIDE] * 5,
        out_specs=(OUTSIDE, OUTSIDE),
        scratch_shapes=[
            pltpu.VMEM(loads.shape, BF16),
            pltpu.VMEM((load_cols, subs), F32),
            pltpu.SMEM(inc.shape, jnp.int32),
            pltpu.SMEM(sizes.shape, jnp.int32),
            pltpu.SemaphoreType.DMA((pieces,)),
            pltpu.SemaphoreType.DMA((1,)),
            pltpu.SemaphoreType.DMA((2,)),
        ],
        compiler_params=room(6),
        name="recover",
    )(inc, sizes, amp, loads, state, diag, phi)


def exchange(parts, axis):
    return lax.all_to_all(parts, axis, 0, 0, tiled=True)


def moved(value, axis, by):
    peers = lax.axis_size(axis)
    return lax.ppermute(value, axis, [(i, (i + by) % peers) for i in range(peers)])


def swapped(value, axis, bits):
    return lax.ppermute(value, axis, [(i, i ^ bits) for i in range(lax.axis_size(axis))])


def body(loads, state, modal_diag, phi, incidence, sizes, factor):
    wide = lax.axis_size(WIDE)
    frows = factor.shape[0]
    others = (1, 3, 2)
    partial, loads_in, phi_in = condense(incidence, sizes, loads, phi, wide, factor.shape[0], 8, 128)
    other = moved(factor, "c", 1)
    own_loads = total_of([exchange(partial, WIDE)], 0)
    own, other = rounded(factor, other, own_loads)
    chip_loads = [own_loads] + [swapped(own_loads, "z", b) for b in others]
    image_part = times_factor(chip_loads, own, other, 512)
    rows = image_part.shape[0]
    image_parts = exchange(image_part.reshape(wide, rows // wide, -1), WIDE)
    image = exchange(total_of([image_parts], wide), WIDE).reshape(rows, -1)
    diag = modal_diag.reshape(-1, BLOCK)
    amp_parts = times_transpose(image, own, other, 4, 128)
    amp_parts = [amp_parts[0]] + [swapped(a, "z", b) for a, b in reversed(list(zip(amp_parts[1:], others)))]
    amp_all = exchange(total_of(amp_parts, wide), WIDE)
    return recover(incidence, sizes, amp_all, loads_in, state, diag, phi_in, 256, 32)


def solution(mesh):
    fine = Mesh(mesh.devices.reshape(4, 4, 4, 2), ("x", "y", "z", "c"))
    wide, narrow = WIDE, ("z", "c")
    return jax.shard_map(
        body,
        mesh=fine,
        in_specs=(
            P(narrow, wide),
            P(narrow, wide),
            P(wide),
            P(wide, None, None),
            P(wide),
            P(wide),
            P(wide, narrow),
        ),
        out_specs=(P(narrow, wide), P(narrow, wide)),
        check_vma=False,
    )
```

```python
import jax
import jax.numpy as jnp
from jax import lax
from jax.experimental import pallas as pl
from jax.experimental.pallas import tpu as pltpu
from jax.sharding import Mesh, PartitionSpec as P

sens_scale = 0.0625
BLOCK = 128
WIDE = ("x", "y")
F32, BF16 = jnp.float32, jnp.bfloat16
OUTSIDE = pl.BlockSpec(memory_space=pltpu.HBM)
INSIDE = pl.BlockSpec(memory_space=pltpu.VMEM)
PAIR = 2 * BLOCK


def outside(array):
    return pltpu.with_memory_space_constraint(array, pltpu.HBM)


def room(mib):
    return pltpu.CompilerParams(vmem_limit_bytes=mib << 20)


def condense(inc, sizes, loads, phi, peers, frows, chunks, unroll):
    load_cols = loads.shape[0]
    tiles = phi.shape[0]
    subs = sizes.shape[0]
    per = frows // BLOCK
    blocks = peers * per
    some = tiles // chunks

    def kernel(inc_hbm, sizes_hbm, loads_hbm, phi_hbm, out_ref, loads_ref, phi_ref, *scratch):
        acc_ref, inc_ref, sizes_ref, loads_sem, phi_sem, scalar_sem = scratch

        def loads_copy(c):
            cols = pl.ds(c * some * BLOCK, some * BLOCK)
            return pltpu.make_async_copy(loads_hbm.at[:, cols], loads_ref.at[:, cols], loads_sem.at[c])

        def phi_copy(c):
            rows = pl.ds(c * some, some)
            return pltpu.make_async_copy(phi_hbm.at[rows], phi_ref.at[rows], phi_sem.at[c])

        inc_copy = pltpu.make_async_copy(inc_hbm, inc_ref, scalar_sem.at[0])
        sizes_copy = pltpu.make_async_copy(sizes_hbm, sizes_ref, scalar_sem.at[1])
        sizes_copy.start()
        inc_copy.start()
        for c in range(chunks):
            loads_copy(c).start()
            phi_copy(c).start()
        acc_ref[...] = jnp.zeros_like(acc_ref)
        sizes_copy.wait()
        live = lax.fori_loop(0, subs, lambda s, n: n + sizes_ref[s], jnp.int32(0), unroll=16)
        inc_copy.wait()

        def part(p, carry):
            for j in range(0, unroll, 2):
                tile = p * unroll + j
                if j % some == 0:
                    c = p * (unroll // some) + j // some
                    loads_copy(c).wait()
                    phi_copy(c).wait()
                cols = pl.multiple_of(tile * BLOCK, PAIR)
                none = jnp.zeros((load_cols, BLOCK), BF16)
                rows = jnp.concatenate(
                    [
                        jnp.concatenate([loads_ref[:, pl.ds(cols, BLOCK)], none], axis=1),
                        jnp.concatenate([none, loads_ref[:, pl.ds(cols + BLOCK, BLOCK)]], axis=1),
                    ],
                    axis=0,
                )
                both = phi_ref[pl.ds(tile, 2)].reshape(PAIR, BLOCK)
                terms = jnp.dot(rows, both, preferred_element_type=F32)
                first, second = terms[:load_cols], terms[load_cols:]
                acc_ref[inc_ref[tile]] += jnp.where(tile < live, first, jnp.zeros_like(first))
                acc_ref[inc_ref[tile + 1]] += jnp.where(tile + 1 < live, second, jnp.zeros_like(second))
            return carry

        lax.fori_loop(0, tiles // unroll, part, 0)
        for b in range(blocks):
            out_ref[b // per, :, (b % per) * BLOCK : (b % per + 1) * BLOCK] = acc_ref[b].astype(BF16)

    return pl.pallas_call(
        kernel,
        out_shape=(
            jax.ShapeDtypeStruct((peers, load_cols, frows), BF16),
            pltpu.VMEM(loads.shape, BF16),
            pltpu.VMEM(phi.shape, BF16),
        ),
        in_specs=[OUTSIDE] * 4,
        out_specs=(INSIDE,) * 3,
        scratch_shapes=[
            pltpu.VMEM((blocks, load_cols, BLOCK), F32),
            pltpu.SMEM(inc.shape, jnp.int32),
            pltpu.SMEM(sizes.shape, jnp.int32),
            pltpu.SemaphoreType.DMA((chunks,)),
            pltpu.SemaphoreType.DMA((chunks,)),
            pltpu.SemaphoreType.DMA((2,)),
        ],
        compiler_params=room(4),
        name="condense",
    )(*[outside(a) for a in (inc, sizes, loads, phi)])


def rounded(own, other, after):
    def kernel(own_ref, other_ref, after_ref, own_out, other_out):
        own_out[...] = own_ref[...].astype(BF16)
        other_out[...] = other_ref[...].astype(BF16)

    return pl.pallas_call(
        kernel,
        out_shape=(pltpu.VMEM(own.shape, BF16), pltpu.VMEM(own.shape, BF16)),
        in_specs=[INSIDE] * 3,
        out_specs=(INSIDE, INSIDE),
        compiler_params=room(4),
        cost_estimate=pl.CostEstimate(flops=2 * own.size, transcendentals=0, bytes_accessed=12 * own.size),
        name="rounded",
    )(own, other, after)


def total_of(parts, copies):
    shape = parts[0].shape[1:] if len(parts) == 1 else parts[0].shape

    def kernel(*refs):
        *part_refs, out_ref = refs
        if len(parts) == 1:
            terms = [part_refs[0][i] for i in range(parts[0].shape[0])]
        else:
            terms = [r[...] for r in part_refs]
        total = terms[0].astype(F32)
        for term in terms[1:]:
            total += term.astype(F32)
        total = total.astype(BF16)
        if copies:
            for i in range(copies):
                out_ref[i] = total
        else:
            out_ref[...] = total

    return pl.pallas_call(
        kernel,
        out_shape=jax.ShapeDtypeStruct((copies, *shape) if copies else shape, BF16),
        in_specs=[INSIDE] * len(parts),
        out_specs=INSIDE,
        compiler_params=room(4),
        name="total_of",
    )(*parts)


def times_factor(parts, own, other, width):
    rows = len(parts) * parts[0].shape[0]
    cols = own.shape[1]

    def kernel(*refs):
        *part_refs, own_ref, other_ref, out_ref = refs
        left = jnp.concatenate([r[...] for r in part_refs], axis=0)
        for at, half_ref in ((0, own_ref), (cols, other_ref)):
            for c in range(0, cols, width):
                product = jnp.dot(left, half_ref[:, c : c + width], preferred_element_type=F32)
                out_ref[:, at + c : at + c + width] = product.astype(BF16)

    return pl.pallas_call(
        kernel,
        out_shape=jax.ShapeDtypeStruct((rows, 2 * cols), BF16),
        in_specs=[INSIDE] * (len(parts) + 2),
        out_specs=INSIDE,
        compiler_params=room(8),
        name="times_factor",
    )(*parts, own, other)


def times_transpose(image, own, other, groups, height):
    rows = image.shape[0]
    frows, cols = own.shape
    group = rows // groups
    contract = (((1,), (1,)), ((), ()))

    def kernel(image_ref, own_ref, other_ref, *outs):
        for c in range(frows // height):
            some = slice(c * height, (c + 1) * height)
            total = lax.dot_general(image_ref[:, :cols], own_ref[some], contract, preferred_element_type=F32)
            total += lax.dot_general(image_ref[:, cols:], other_ref[some], contract, preferred_element_type=F32)
            for g in range(groups):
                outs[g][:, some] = total[g * group : (g + 1) * group].astype(BF16)

    return pl.pallas_call(
        kernel,
        out_shape=[jax.ShapeDtypeStruct((group, frows), BF16)] * groups,
        in_specs=[INSIDE] * 3,
        out_specs=[INSIDE] * groups,
        compiler_params=room(8),
        name="times_transpose",
    )(image, own, other)


def recover(inc, sizes, amp, loads, state, diag, phi, unroll, some):
    load_cols = loads.shape[0]
    tiles = phi.shape[0]
    subs = sizes.shape[0]
    per = amp.shape[2] // BLOCK
    parts = tiles // unroll
    pieces = tiles // some
    contract = (((1,), (1,)), ((), ()))

    def kernel(inc_hbm, sizes_hbm, amp_ref, loads_ref, state_ref, diag_ref, phi_ref, adj_hbm, sens_hbm, *scratch):
        adj_ref, sens_ref, inc_ref, sizes_ref, sem, sens_sem, scalar_sem = scratch
        inc_copy = pltpu.make_async_copy(inc_hbm, inc_ref, scalar_sem.at[0])
        sizes_copy = pltpu.make_async_copy(sizes_hbm, sizes_ref, scalar_sem.at[1])
        inc_copy.start()
        sizes_copy.start()
        lane = lax.broadcasted_iota(jnp.int32, (load_cols, subs), 1)
        inc_copy.wait()
        sizes_copy.wait()

        def block(tile):
            at = inc_ref[tile]
            cols = pl.multiple_of(lax.rem(at, per) * BLOCK, BLOCK)
            return amp_ref[lax.div(at, per), :, pl.ds(cols, BLOCK)]

        def adj_copy(p):
            cols = pl.ds(pl.multiple_of(p * some * BLOCK, BLOCK), some * BLOCK)
            return pltpu.make_async_copy(adj_ref.at[:, cols], adj_hbm.at[:, cols], sem.at[p])

        def part(p, carry):
            owner, end, sens = carry
            for j in range(0, unroll, 2):
                tile = p * unroll + j
                none = jnp.zeros((load_cols, BLOCK), BF16)
                rows = jnp.concatenate(
                    [jnp.concatenate([block(tile), none], axis=1), jnp.concatenate([none, block(tile + 1)], axis=1)], axis=0
                )
                both = jnp.concatenate([phi_ref[tile], phi_ref[tile + 1]], axis=1)
                product = lax.dot_general(rows, both, contract, preferred_element_type=F32)
                couplings = (product[:load_cols], product[load_cols:])
                for q, coupling in enumerate(couplings):
                    past = (tile + q >= end) & (owner < subs)
                    owner = jnp.where(past, owner + 1, owner)
                    end = jnp.where(past & (owner < subs), end + sizes_ref[jnp.minimum(owner, subs - 1)], end)
                    cols = pl.ds(pl.multiple_of((tile + q) * BLOCK, BLOCK), BLOCK)
                    response = diag_ref[pl.ds(tile + q, 1), :] * loads_ref[:, cols].astype(F32) + coupling
                    response = jnp.where(owner < subs, response, jnp.zeros_like(response))
                    adj_ref[:, cols] = response.astype(BF16)
                    total = jnp.sum(response * state_ref[:, cols].astype(F32), axis=1, keepdims=True)
                    sens = sens + jnp.where(lane == owner, total, jnp.zeros_like(sens))
                if (j + 2) % some == 0:
                    adj_copy(p * (unroll // some) + j // some).start()
            return owner, end, sens

        start = (jnp.int32(0), sizes_ref[0], jnp.zeros((load_cols, subs), F32))
        _, _, sens = lax.fori_loop(0, parts, part, start)
        sens_ref[...] = sens * sens_scale
        sens_copy = pltpu.make_async_copy(sens_ref, sens_hbm, sens_sem.at[0])
        sens_copy.start()
        for p in range(pieces):
            adj_copy(p).wait()
        sens_copy.wait()

    return pl.pallas_call(
        kernel,
        out_shape=(
            jax.ShapeDtypeStruct(loads.shape, BF16),
            jax.ShapeDtypeStruct((load_cols, subs), F32),
        ),
        in_specs=[OUTSIDE] * 2 + [INSIDE] * 5,
        out_specs=(OUTSIDE, OUTSIDE),
        scratch_shapes=[
            pltpu.VMEM(loads.shape, BF16),
            pltpu.VMEM((load_cols, subs), F32),
            pltpu.SMEM(inc.shape, jnp.int32),
            pltpu.SMEM(sizes.shape, jnp.int32),
            pltpu.SemaphoreType.DMA((pieces,)),
            pltpu.SemaphoreType.DMA((1,)),
            pltpu.SemaphoreType.DMA((2,)),
        ],
        compiler_params=room(6),
        name="recover",
    )(inc, sizes, amp, loads, state, diag, phi)


def exchange(parts, axis):
    return lax.all_to_all(parts, axis, 0, 0, tiled=True)


def moved(value, axis, by):
    peers = lax.axis_size(axis)
    return lax.ppermute(value, axis, [(i, (i + by) % peers) for i in range(peers)])


def swapped(value, axis, bits):
    return lax.ppermute(value, axis, [(i, i ^ bits) for i in range(lax.axis_size(axis))])


def body(loads, state, modal_diag, phi, incidence, sizes, factor):
    wide = lax.axis_size(WIDE)
    frows = factor.shape[0]
    others = (1, 3, 2)
    partial, loads_in, phi_in = condense(incidence, sizes, loads, phi, wide, factor.shape[0], 8, 128)
    other = moved(factor, "c", 1)
    own_loads = total_of([exchange(partial, WIDE)], 0)
    own, other = rounded(factor, other, own_loads)
    chip_loads = [own_loads] + [swapped(own_loads, "z", b) for b in others]
    image_part = times_factor(chip_loads, own, other, 512)
    rows = image_part.shape[0]
    image_parts = exchange(image_part.reshape(wide, rows // wide, -1), WIDE)
    image = exchange(total_of([image_parts], wide), WIDE).reshape(rows, -1)
    diag = modal_diag.reshape(-1, BLOCK)
    amp_parts = times_transpose(image, own, other, 4, 128)
    amp_parts = [amp_parts[0]] + [swapped(a, "z", b) for a, b in reversed(list(zip(amp_parts[1:], others)))]
    amp_all = exchange(total_of(amp_parts, wide), WIDE)
    return recover(incidence, sizes, amp_all, loads_in, state, diag, phi_in, 256, 32)


def solution(mesh):
    fine = Mesh(mesh.devices.reshape(4, 4, 4, 2), ("x", "y", "z", "c"))
    wide, narrow = WIDE, ("z", "c")
    return jax.shard_map(
        body,
        mesh=fine,
        in_specs=(
            P(narrow, wide),
            P(narrow, wide),
            P(wide),
            P(wide, None, None),
            P(wide),
            P(wide),
            P(wide, narrow),
        ),
        out_specs=(P(narrow, wide), P(narrow, wide)),
        check_vma=False,
    )
```
